512 devices in a mesh: slab: 64 (over z, x_hi, core), band: 8 (over y, x_lo).
Axes of the slice: x: 4 (x_hi: 2, x_lo: 2; x = x_hi * 2 + x_lo), y: 4, z: 16, core: 2. Of those that a mesh axis runs over, the one named last changes fastest.
Arguments:
- hamiltonian: bfloat16 [512, 7, 128, 128], P('slab', None, 'band'), may hold values from -0.1875 to 0.1875
- neighbors: int32 [512, 7], P('slab'), may hold values from 0 to 11, as said below
- orbitals: bfloat16 [65536, 1024], P('slab', 'band'), may hold values from -6 to 6
Outputs:
- residual: bfloat16 [65536, 1024], P(('slab', 'band'))
The draws below stay inside these ranges and needn't reach their ends.
Inputs may be any that keep to these rules, and one draw needn't show every extreme that they name: `neighbors`: window positions 0 to 1 are the last 2 elements of the slab below (periodic), 2 to 9 the slab's own elements, the rest the first 2 elements of the slab above. A slab's elements are in layers of 2; each block row names, in an order of its own, itself, the element 2 positions below and above it in the window, and four elements of its own layer (repeats possible).
All inputs are finite; a program needn't handle non-finite values.
Results may differ from the reference program's by a relative error of at most 0.012.
Values may be sent and summed in bfloat16 or wider, within the bound.
No kernel may reach another device: no remote copies, remote signals or barrier semaphores. Data moves between devices by JAX's collectives and lax.ppermute only.
A program may use at most 64 MiB of HBM per device.

```python
import math
import jax
import jax.numpy as jnp

TILE = 128
BANDS = 1024
FACE = 2
BLK_DEV = 8
NBLK = 512
ROWS = 65536


def draw_neighbors(key, part):
    block_index = jnp.arange(NBLK, dtype=jnp.int32)
    within = block_index % BLK_DEV
    layer_base = FACE + within // FACE * FACE
    plane_key = jax.random.fold_in(key, 11)
    order_key = jax.random.fold_in(key, 23)
    inplane = layer_base[:, None] + jax.random.randint(plane_key, (NBLK, 4), 0, FACE, dtype=jnp.int32)
    itself = (FACE + within)[:, None]
    below = within[:, None]
    above = (2 * FACE + within)[:, None]
    columns = jnp.concatenate([itself, below, above, inplane], axis=1).astype(jnp.int32)
    row_keys = jax.random.split(order_key, NBLK)
    orders = jax.vmap(lambda k: jax.random.permutation(k, 7))(row_keys).astype(jnp.int32)
    return jnp.take_along_axis(columns, orders, axis=1).astype(jnp.int32)


def levels(own_key, shape, shards, smallest, largest):
    level, own = 1.0, jax.random.fold_in(own_key, 6)
    for position, blocks in shards:
        heights = jnp.exp(jax.random.uniform(jax.random.fold_in(own, position), (blocks,), jnp.float32, smallest / len(shards), largest / len(shards)))
        level = level * jnp.repeat(heights, shape[position] // blocks).reshape([-1 if axis == position else 1 for axis in range(len(shape))])
    return level


def centred(stream_key, dims, deviation, most, pieces=(), kind=jnp.bfloat16):
    entries = jax.random.normal(stream_key, dims, jnp.float32) * deviation
    if len(pieces) > 0:
        entries = levels(stream_key, dims, pieces, -0.22, 0.18) * entries
    return jnp.clip(entries, min=-most, max=most).astype(kind)


def setup_inputs(seed: int = 0) -> dict:
    key_list = jax.random.split(jax.random.key(seed), 4)
    return {
        "hamiltonian": centred(key_list[0], (NBLK, 7, TILE, TILE), (7 * TILE) ** -0.5, 0.1875, ((0, 64), (2, 8))),
        "neighbors": draw_neighbors(jax.random.fold_in(key_list[3], 71), 0),
        "orbitals": centred(key_list[2], (ROWS, BANDS), 1.0, 6.0, ((0, 64), (1, 8))),
    }


def reference(hamiltonian, neighbors, orbitals):
    nblk = hamiltonian.shape[0]
    tile_size = hamiltonian.shape[2]
    bands_all = orbitals.shape[1]
    block_index = jnp.arange(nblk, dtype=jnp.int32)
    slab_start = block_index // BLK_DEV * BLK_DEV
    global_cols = ((slab_start[:, None] - FACE + neighbors) % nblk).astype(jnp.int32)

    def apply(vector):
        blocks = vector.reshape(nblk, tile_size, bands_all).astype(jnp.float32)
        total = jnp.zeros((nblk, tile_size, bands_all), jnp.float32)
        for slot in range(7):
            total = total + jnp.einsum('rab,rbc->rac', hamiltonian[:, slot].astype(jnp.float32), blocks[global_cols[:, slot]])
        return total.reshape(nblk * tile_size, bands_all)
    first = apply(orbitals).astype(jnp.bfloat16)
    second = (2.0 * apply(first) - orbitals.astype(jnp.float32)).astype(jnp.bfloat16)
    third = (2.0 * apply(second) - first.astype(jnp.float32)).astype(jnp.bfloat16)
    applied = apply(third).astype(jnp.bfloat16)
    gram_scale = 1.0 / math.sqrt(float(nblk * tile_size) * float(bands_all))
    gram_full = (jnp.dot(third.T, applied, preferred_element_type=jnp.float32) * gram_scale).astype(jnp.bfloat16)
    mixed = jnp.dot(third, gram_full, preferred_element_type=jnp.float32)
    return (applied.astype(jnp.float32) - mixed).astype(jnp.bfloat16)
```

```python
import functools
import math

import jax
import jax.numpy as jnp
import numpy as np
from jax import lax
from jax.experimental import pallas as pl
from jax.experimental.pallas import tpu as pltpu
from jax.sharding import Mesh
from jax.sharding import PartitionSpec as P

SLAB = ("z2", "z1", "xh", "core")
BAND = ("y", "xl")
NEAR = ("z1", "xh", "core")
FACE = 2
F32 = jnp.float32
BF16 = jnp.bfloat16

VMEM = pl.BlockSpec(memory_space=pltpu.VMEM)
SMEM = pl.BlockSpec(memory_space=pltpu.SMEM)


def dot(a, b, dims=((1,), (0,))):
    return lax.dot_general(a, b, (dims, ((), ())), preferred_element_type=F32)


def call(kernel, outs, args, scratch=(), smem=0):
    return pl.pallas_call(
        kernel,
        out_shape=[jax.ShapeDtypeStruct(shape, BF16) for shape in outs],
        in_specs=[SMEM] * smem + [VMEM] * (len(args) - smem),
        out_specs=[VMEM] * len(outs),
        scratch_shapes=list(scratch),
    )(*args)


def combine_kernel(nbr, ham, out):
    blocks, slots = ham.shape[0], ham.shape[1]
    width = ham.shape[3]
    for r in range(blocks):
        layer = FACE + r // FACE * FACE
        for k, position in enumerate((r, layer, layer + 1, r + 2 * FACE)):
            total = jnp.zeros(ham.shape[2:], F32)
            for j in range(slots):
                keep = (nbr[r, j] == position).astype(F32)
                total = total + keep * ham[r, j].astype(F32)
            total = total.astype(BF16)
            for copy in range(out.shape[0]):
                out[copy, r, :, k * width : (k + 1) * width] = total


def apply_kernel(prior, copies, core, ham, vec, from_a, from_b, *rest):
    before = rest[0] if prior else None
    rest = rest[1:] if prior else rest
    ext = rest[-1]
    edge = from_a.shape[0]
    rows = vec.shape[0]
    tile = edge // FACE
    c = core[0]
    ext[edge : edge + rows] = vec[...]
    ext[pl.ds(pl.multiple_of((1 - c) * (edge + rows), edge), edge)] = from_a[...]
    ext[pl.ds(pl.multiple_of(c * (edge + rows), edge), edge)] = from_b[...]
    out = rest[0]
    for r in range(rows // tile):
        layer = FACE + r // FACE * FACE
        lhs = ham[:, r].reshape(tile, 4 * tile)
        rhs = jnp.concatenate(
            [
                ext[r * tile : (r + 1) * tile],
                ext[layer * tile : (layer + FACE) * tile],
                ext[(r + 2 * FACE) * tile : (r + 2 * FACE + 1) * tile],
            ],
            axis=0,
        )
        value = dot(lhs, rhs)
        here = slice(r * tile, (r + 1) * tile)
        if prior:
            value = 2.0 * value - before[here].astype(F32)
        value = value.astype(BF16)
        out[here] = value
        if copies:
            for copy in range(copies):
                rest[3][copy, here] = value
    if len(rest) > 2:
        rest[1][...] = out[pl.ds(pl.multiple_of((1 - c) * (rows - edge), edge), edge)]
        rest[2][...] = out[pl.ds(pl.multiple_of(c * (rows - edge), edge), edge)]


def gram_kernel(third, own, other, out):
    right = jnp.concatenate([own[...], other[...]], axis=1)
    share = out.shape[1]
    per = third.shape[2] // share
    for y in range(third.shape[0]):
        block = dot(third[y], right, ((0,), (0,))).astype(BF16)
        for i in range(per):
            out[y * per + i] = block[i * share : (i + 1) * share]


def sum_kernel(scale, parts, out):
    total = parts[0].astype(F32)
    for i in range(1, parts.shape[0]):
        total = total + parts[i].astype(F32)
    if scale is not None:
        total = total * scale
    total = total.astype(BF16)
    for copy in range(out.shape[0]):
        out[copy] = total


def mixed_kernel(third, gram, applied, out):
    strips, height = out.shape[0], out.shape[1]
    width = third.shape[2]
    depth = third.shape[0] * width
    weights = gram[...].reshape(depth, gram.shape[2])
    for s in range(strips):
        here = slice(s * height, (s + 1) * height)
        left = jnp.concatenate([third[y, here] for y in range(third.shape[0])], axis=1)
        value = dot(left, weights)
        out[s, :, :width] = (applied[here].astype(F32) - value[:, :width]).astype(BF16)
        out[s, :, width:] = (-value[:, width:]).astype(BF16)


def final_kernel(parts, out):
    width = parts.shape[2] // 2
    for b in range(parts.shape[0]):
        value = parts[b, :, :width].astype(F32) + parts[b ^ 1, :, width:].astype(F32)
        out[:, b * width : (b + 1) * width] = value.astype(BF16)


def gather(copies, axes):
    return lax.all_to_all(copies, axes, 0, 0, tiled=True)


def swap(near, far):
    count = lax.axis_size(SLAB)
    pairs = [(s, (s + 1) % count if s % 2 else (s - 1) % count) for s in range(count)]
    return (
        lax.ppermute(near, "core", [(0, 1), (1, 0)]),
        lax.ppermute(far, SLAB, pairs),
    )


def body(hamiltonian, neighbors, orbitals):
    blocks, _, strip, tile = hamiltonian.shape
    rows, width = orbitals.shape
    edge = FACE * tile
    ny, nband, near, far = (lax.axis_size(a) for a in ("y", BAND, NEAR, "z2"))
    core = lax.axis_index("core")
    scalar = core.astype(jnp.int32).reshape(1)

    (shares,) = call(
        combine_kernel, [(nband, blocks, strip, 4 * tile)], (neighbors, hamiltonian), smem=1
    )
    tiles = gather(shares, BAND)
    received = swap(
        lax.dynamic_slice_in_dim(orbitals, (1 - core) * (rows - edge), edge, 0),
        lax.dynamic_slice_in_dim(orbitals, core * (rows - edge), edge, 0),
    )

    def apply(vec, received, before=None, copies=0, edges=True):
        args = (scalar, tiles, vec, *received) + (() if before is None else (before,))
        outs = [(rows, width)] + [(edge, width)] * (2 if edges else 0)
        if copies:
            outs.append((copies, rows, width))
        return call(
            functools.partial(apply_kernel, before is not None, copies),
            outs,
            args,
            (pltpu.VMEM((rows + 2 * edge, width), BF16),),
            smem=1,
        )

    first, *edges = apply(orbitals, received)
    second, *edges = apply(first, swap(*edges), orbitals)
    third, *edges, copies = apply(second, swap(*edges), first, copies=ny)
    third_all = gather(copies, "y")
    (applied,) = apply(third, swap(*edges), edges=False)
    other = lax.ppermute(applied, "xl", [(0, 1), (1, 0)])

    rows_all = rows * lax.axis_size(SLAB)
    scale = 1.0 / math.sqrt(float(rows_all) * float(width * nband))
    share = ny * width // near
    (partial_gram,) = call(gram_kernel, [(near, share, 2 * width)], (third_all, applied, other))
    (summed,) = call(
        functools.partial(sum_kernel, None),
        [(far, share, 2 * width)],
        (gather(partial_gram, NEAR),),
    )
    (scaled,) = call(
        functools.partial(sum_kernel, scale),
        [(near, share, 2 * width)],
        (gather(summed, "z2"),),
    )
    gram = gather(scaled, NEAR)
    (partial_out,) = call(
        mixed_kernel, [(nband, rows // nband, 2 * width)], (third_all, gram, applied)
    )
    (out,) = call(final_kernel, [(rows // nband, nband * width)], (gather(partial_out, BAND),))
    return out


def solution(mesh):
    slabs = mesh.shape["slab"]
    fine = Mesh(
        np.asarray(mesh.devices).reshape(slabs // 16, 4, 2, 2, mesh.shape["band"] // 2, 2),
        SLAB + BAND,
    )
    in_specs = (P(SLAB, None, BAND, None), P(SLAB, None), P(SLAB, BAND))
    out_specs = P(SLAB + BAND, None)
    return jax.shard_map(body, mesh=fine, in_specs=in_specs, out_specs=out_specs, check_vma=False)
```

```python
import functools
import math

import jax
import jax.numpy as jnp
import numpy as np
from jax import lax
from jax.experimental import pallas as pl
from jax.experimental.pallas import tpu as pltpu
from jax.sharding import Mesh
from jax.sharding import PartitionSpec as P

SLAB = ("z2", "z1", "xh", "core")
BAND = ("y", "xl")
NEAR = ("z1", "xh", "core")
FACE = 2
F32 = jnp.float32
BF16 = jnp.bfloat16

VMEM = pl.BlockSpec(memory_space=pltpu.VMEM)
SMEM = pl.BlockSpec(memory_space=pltpu.SMEM)


def dot(a, b, dims=((1,), (0,))):
    return lax.dot_general(a, b, (dims, ((), ())), preferred_element_type=F32)


def call(kernel, outs, args, scratch=(), smem=0, far=(), last=False):
    args = [
        x if i < smem or i in far else pltpu.with_memory_space_constraint(x, pltpu.VMEM)
        for i, x in enumerate(args)
    ]
    make = jax.ShapeDtypeStruct if last else pltpu.VMEM
    return pl.pallas_call(
        kernel,
        out_shape=[make(shape, BF16) for shape in outs],
        in_specs=[SMEM] * smem + [VMEM] * (len(args) - smem),
        out_specs=[VMEM] * len(outs),
        scratch_shapes=list(scratch),
    )(*args)


def combine_kernel(nbr, ham, out):
    blocks, slots = ham.shape[0], ham.shape[1]
    width = ham.shape[3]
    for r in range(blocks):
        layer = FACE + r // FACE * FACE
        for k, position in enumerate((r, layer, layer + 1, r + 2 * FACE)):
            total = jnp.zeros(ham.shape[2:], F32)
            for j in range(slots):
                keep = (nbr[r, j] == position).astype(F32)
                total = total + keep * ham[r, j].astype(F32)
            total = total.astype(BF16)
            for copy in range(out.shape[0]):
                out[copy, r, :, k * width : (k + 1) * width] = total


def apply_kernel(prior, copies, core, ham, vec, from_far, from_near, *rest):
    before = rest[0] if prior else None
    rest = rest[1:] if prior else rest
    ext = rest[-1]
    edge = from_far.shape[0]
    rows = vec.shape[0]
    tile = edge // FACE
    c = core[0]
    ext[edge : edge + rows] = vec[...]
    ext[pl.ds(pl.multiple_of((1 - c) * (edge + rows), edge), edge)] = from_near[...]
    ext[pl.ds(pl.multiple_of(c * (edge + rows), edge), edge)] = from_far[...]
    out = rest[0]
    for r in range(rows // tile):
        layer = FACE + r // FACE * FACE
        lhs = ham[:, r].reshape(tile, 4 * tile)
        rhs = jnp.concatenate(
            [
                ext[r * tile : (r + 1) * tile],
                ext[layer * tile : (layer + FACE) * tile],
                ext[(r + 2 * FACE) * tile : (r + 2 * FACE + 1) * tile],
            ],
            axis=0,
        )
        value = dot(lhs, rhs)
        here = slice(r * tile, (r + 1) * tile)
        if prior:
            value = 2.0 * value - before[here].astype(F32)
        value = value.astype(BF16)
        out[here] = value
        if copies:
            for copy in range(copies):
                rest[3][copy, here] = value
    if len(rest) > 2:
        rest[1][...] = out[pl.ds(pl.multiple_of(c * (rows - edge), edge), edge)]
        rest[2][...] = out[pl.ds(pl.multiple_of((1 - c) * (rows - edge), edge), edge)]


def gram_kernel(third, own, other, out):
    right = jnp.concatenate([own[...], other[...]], axis=1)
    share = out.shape[1]
    per = third.shape[2] // share
    for y in range(third.shape[0]):
        block = dot(third[y], right, ((0,), (0,))).astype(BF16)
        for i in range(per):
            out[y * per + i] = block[i * share : (i + 1) * share]


def sum_kernel(scale, parts, out):
    total = parts[0].astype(F32)
    for i in range(1, parts.shape[0]):
        total = total + parts[i].astype(F32)
    if scale is not None:
        total = total * scale
    total = total.astype(BF16)
    for copy in range(out.shape[0]):
        out[copy] = total


def mixed_kernel(third, gram, applied, out):
    strips, height = out.shape[0], out.shape[1]
    width = third.shape[2]
    depth = third.shape[0] * width
    weights = gram[...].reshape(depth, gram.shape[2])
    for s in range(strips):
        here = slice(s * height, (s + 1) * height)
        left = jnp.concatenate([third[y, here] for y in range(third.shape[0])], axis=1)
        value = dot(left, weights)
        out[s, :, :width] = (applied[here].astype(F32) - value[:, :width]).astype(BF16)
        out[s, :, width:] = (-value[:, width:]).astype(BF16)


def final_kernel(parts, out):
    width = parts.shape[2] // 2
    for b in range(parts.shape[0]):
        value = parts[b, :, :width].astype(F32) + parts[b ^ 1, :, width:].astype(F32)
        out[:, b * width : (b + 1) * width] = value.astype(BF16)


def gather(copies, axes):
    return lax.all_to_all(copies, axes, 0, 0, tiled=True)


def swap(far, near):
    count = lax.axis_size(SLAB)
    pairs = [(s, (s + 1) % count if s % 2 else (s - 1) % count) for s in range(count)]
    from_far = lax.ppermute(far, SLAB, pairs)
    return from_far, lax.ppermute(near, "core", [(0, 1), (1, 0)])


def body(hamiltonian, neighbors, orbitals):
    blocks, _, strip, tile = hamiltonian.shape
    rows, width = orbitals.shape
    edge = FACE * tile
    ny, nband, near, far = (lax.axis_size(a) for a in ("y", BAND, NEAR, "z2"))
    core = lax.axis_index("core")
    scalar = core.astype(jnp.int32).reshape(1)

    (shares,) = call(
        combine_kernel, [(nband, blocks, strip, 4 * tile)], (neighbors, hamiltonian), smem=1, far=(1,)
    )
    tiles = gather(shares, BAND)
    received = swap(
        lax.dynamic_slice_in_dim(orbitals, core * (rows - edge), edge, 0),
        lax.dynamic_slice_in_dim(orbitals, (1 - core) * (rows - edge), edge, 0),
    )

    def apply(vec, received, before=None, copies=0, edges=True):
        args = (scalar, tiles, vec, *received) + (() if before is None else (before,))
        outs = [(rows, width)] + [(edge, width)] * (2 if edges else 0)
        if copies:
            outs.append((copies, rows, width))
        return call(
            functools.partial(apply_kernel, before is not None, copies),
            outs,
            args,
            (pltpu.VMEM((rows + 2 * edge, width), BF16),),
            smem=1,
        )

    first, *edges = apply(orbitals, received)
    second, *edges = apply(first, swap(*edges), orbitals)
    third, *edges, copies = apply(second, swap(*edges), first, copies=ny)
    third_all = gather(copies, "y")
    (applied,) = apply(third, swap(*edges), edges=False)
    other = lax.ppermute(applied, "xl", [(0, 1), (1, 0)])

    rows_all = rows * lax.axis_size(SLAB)
    scale = 1.0 / math.sqrt(float(rows_all) * float(width * nband))
    share = ny * width // near
    (partial_gram,) = call(gram_kernel, [(near, share, 2 * width)], (third_all, applied, other))
    (summed,) = call(
        functools.partial(sum_kernel, None),
        [(far, share, 2 * width)],
        (gather(partial_gram, NEAR),),
    )
    (scaled,) = call(
        functools.partial(sum_kernel, scale),
        [(near, share, 2 * width)],
        (gather(summed, "z2"),),
    )
    gram = gather(scaled, NEAR)
    (partial_out,) = call(
        mixed_kernel, [(nband, rows // nband, 2 * width)], (third_all, gram, applied)
    )
    (out,) = call(
        final_kernel, [(rows // nband, nband * width)], (gather(partial_out, BAND),), last=True
    )
    return out


def solution(mesh):
    slabs = mesh.shape["slab"]
    fine = Mesh(
        np.asarray(mesh.devices).reshape(slabs // 16, 4, 2, 2, mesh.shape["band"] // 2, 2),
        SLAB + BAND,
    )
    in_specs = (P(SLAB, None, BAND, None), P(SLAB, None), P(SLAB, BAND))
    out_specs = P(SLAB + BAND, None)
    return jax.shard_map(body, mesh=fine, in_specs=in_specs, out_specs=out_specs, check_vma=False)
```

```python
import functools
import math

import jax
import jax.numpy as jnp
import numpy as np
from jax import lax
from jax.experimental import pallas as pl
from jax.experimental.pallas import tpu as pltpu
from jax.sharding import Mesh
from jax.sharding import PartitionSpec as P

SLAB = ("z2", "z1", "xh", "core")
BAND = ("y", "xl")
NEAR = ("z1", "xh", "core")
FACE = 2
F32 = jnp.float32
BF16 = jnp.bfloat16

VMEM = pl.BlockSpec(memory_space=pltpu.VMEM)
SMEM = pl.BlockSpec(memory_space=pltpu.SMEM)
HBM = pl.BlockSpec(memory_space=pltpu.MemorySpace.HBM)


def dot(a, b, dims=((1,), (0,))):
    return lax.dot_general(a, b, (dims, ((), ())), preferred_element_type=F32)


def call(kernel, outs, args, scratch=(), smem=0, far=(), far_outs=(), last=False):
    args = [
        x if i < smem or i in far else pltpu.with_memory_space_constraint(x, pltpu.VMEM)
        for i, x in enumerate(args)
    ]
    spaces = [HBM if i in far_outs else VMEM for i in range(len(outs))]
    plain = [last or i in far_outs for i in range(len(outs))]
    return pl.pallas_call(
        kernel,
        out_shape=[
            (jax.ShapeDtypeStruct if p else pltpu.VMEM)(shape, BF16) for p, shape in zip(plain, outs)
        ],
        in_specs=[SMEM] * smem + [VMEM] * (len(args) - smem),
        out_specs=spaces,
        scratch_shapes=list(scratch),
    )(*args)


def combine_kernel(which, nbr, ham, *refs):
    out = refs[-1]
    slots, width = ham.shape[1], ham.shape[3]
    for i, r in enumerate(which):
        layer = FACE + r // FACE * FACE
        for k, position in enumerate((r, layer, layer + 1, r + 2 * FACE)):
            total = jnp.zeros(ham.shape[2:], F32)
            for j in range(slots):
                keep = (nbr[r, j] == position).astype(F32)
                total = total + keep * ham[r, j].astype(F32)
            total = total.astype(BF16)
            for copy in range(out.shape[0]):
                out[copy, i, :, k * width : (k + 1) * width] = total


def product(ham, i, r, ext):
    tile = ham.shape[3] // 4
    layer = FACE + r // FACE * FACE
    rhs = jnp.concatenate(
        [
            ext[r * tile : (r + 1) * tile],
            ext[layer * tile : (layer + FACE) * tile],
            ext[(r + 2 * FACE) * tile : (r + 2 * FACE + 1) * tile],
        ],
        axis=0,
    )
    return dot(ham[:, i].reshape(tile, 4 * tile), rhs)


def fill_halo(core, ext, from_far, from_near):
    edge = from_far.shape[0]
    last = ext.shape[0] - edge
    c = core[0]
    ext[pl.ds(pl.multiple_of(c * last, edge), edge)] = from_far[...]
    ext[pl.ds(pl.multiple_of((1 - c) * last, edge), edge)] = from_near[...]


def outer_kernel(outer, core, ham, vec, from_far, from_near, out, far, near, ext):
    edge, rows = from_far.shape[0], vec.shape[0]
    tile = edge // FACE
    ext[edge : edge + rows] = vec[...]
    fill_halo(core, ext, from_far, from_near)
    for i, r in enumerate(outer):
        out[i * tile : (i + 1) * tile] = product(ham, i, r, ext).astype(BF16)
    c = core[0]
    far[...] = out[pl.ds(pl.multiple_of(c * edge, edge), edge)]
    near[...] = out[pl.ds(pl.multiple_of((1 - c) * edge, edge), edge)]


def step(outer, inner, ham_outer, ham_inner, ext, before, out):
    tile = ham_outer.shape[3] // 4
    for which, ham in ((outer, ham_outer), (inner, ham_inner)):
        for i, r in enumerate(which):
            here = slice(r * tile, (r + 1) * tile)
            value = product(ham, i, r, ext)
            if before is not None:
                value = 2.0 * value - before[here].astype(F32)
            out[here] = value.astype(BF16)


def edges_out(core, out, far, near):
    edge = far.shape[0]
    last = out.shape[0] - edge
    c = core[0]
    far[...] = out[pl.ds(pl.multiple_of(c * last, edge), edge)]
    near[...] = out[pl.ds(pl.multiple_of((1 - c) * last, edge), edge)]


def second_kernel(
    outer, inner, core, ham_outer, ham_inner, vec, first_outer, from_far, from_near,
    first, second, far, near, ext,
):
    edge, rows = from_far.shape[0], vec.shape[0]
    tile = edge // FACE
    ext[edge : edge + rows] = vec[...]
    for i, r in enumerate(outer):
        first[r * tile : (r + 1) * tile] = first_outer[i * tile : (i + 1) * tile]
    for i, r in enumerate(inner):
        first[r * tile : (r + 1) * tile] = product(ham_inner, i, r, ext).astype(BF16)
    ext[edge : edge + rows] = first[...]
    fill_halo(core, ext, from_far, from_near)
    step(outer, inner, ham_outer, ham_inner, ext, vec, second)
    edges_out(core, second, far, near)


def third_kernel(
    outer, inner, core, ham_outer, ham_inner, vec, before, from_far, from_near,
    out, copies, far, near, ext, sems,
):
    edge, rows = from_far.shape[0], vec.shape[0]
    ext[edge : edge + rows] = vec[...]
    fill_halo(core, ext, from_far, from_near)
    step(outer, inner, ham_outer, ham_inner, ext, before, out)
    sends = [pltpu.make_async_copy(out, copies.at[i], sems.at[i]) for i in range(copies.shape[0])]
    for send in sends:
        send.start()
    edges_out(core, out, far, near)
    for send in sends:
        send.wait()


def applied_kernel(
    outer, inner, core, ham_outer, ham_inner, vec, from_far, from_near, out, ext
):
    edge, rows = from_far.shape[0], vec.shape[0]
    ext[edge : edge + rows] = vec[...]
    fill_halo(core, ext, from_far, from_near)
    step(outer, inner, ham_outer, ham_inner, ext, None, out)


def gram_kernel(third, own, other, out):
    share = out.shape[1]
    per = third.shape[2] // share
    right = jnp.concatenate([own[...], other[...]], axis=1)
    for y in range(third.shape[0]):
        block = dot(third[y], right, ((0,), (0,))).astype(BF16)
        for i in range(per):
            out[y * per + i] = block[i * share : (i + 1) * share]


def sum_kernel(scale, parts, out):
    total = parts[0].astype(F32)
    for i in range(1, parts.shape[0]):
        total = total + parts[i].astype(F32)
    if scale is not None:
        total = total * scale
    total = total.astype(BF16)
    for copy in range(out.shape[0]):
        out[copy] = total


def mixed_kernel(third, gram, applied, out):
    strips, height = out.shape[0], out.shape[1]
    width = third.shape[2]
    depth = third.shape[0] * width
    weights = gram[...].reshape(depth, gram.shape[2])
    for s in range(strips):
        here = slice(s * height, (s + 1) * height)
        left = jnp.concatenate([third[y, here] for y in range(third.shape[0])], axis=1)
        value = dot(left, weights)
        out[s, :, :width] = (applied[here].astype(F32) - value[:, :width]).astype(BF16)
        out[s, :, width:] = (-value[:, width:]).astype(BF16)


def final_kernel(parts, out):
    width = parts.shape[2] // 2
    for b in range(parts.shape[0]):
        value = parts[b, :, :width].astype(F32) + parts[b ^ 1, :, width:].astype(F32)
        out[:, b * width : (b + 1) * width] = value.astype(BF16)


def gather(copies, axes):
    return lax.all_to_all(copies, axes, 0, 0, tiled=True)


def swap(far, near):
    count = lax.axis_size(SLAB)
    pairs = [(s, (s + 1) % count if s % 2 else (s - 1) % count) for s in range(count)]
    from_far = lax.ppermute(far, SLAB, pairs)
    return from_far, lax.ppermute(near, "core", [(0, 1), (1, 0)])


def body(hamiltonian, neighbors, orbitals):
    blocks, _, strip, tile = hamiltonian.shape
    rows, width = orbitals.shape
    edge = FACE * tile
    ny, nband, near, far = (lax.axis_size(a) for a in ("y", BAND, NEAR, "z2"))
    core = lax.axis_index("core")
    scalar = core.astype(jnp.int32).reshape(1)

    outer = (*range(FACE), *range(blocks - FACE, blocks))
    inner = tuple(range(FACE, blocks - FACE))

    def shares(which, *after):
        outs = [(nband, len(which), strip, 4 * tile)]
        kernel = functools.partial(combine_kernel, which)
        return call(kernel, outs, (neighbors, hamiltonian, *after), smem=1, far=(1,))[0]

    def run(kernel, outs, args, scratch=(), far_outs=()):
        ext = pltpu.VMEM((rows + 2 * edge, width), BF16)
        return call(kernel, outs, (scalar, *args), (ext, *scratch), smem=1, far_outs=far_outs)

    whole, face = (rows, width), (edge, width)
    ham_outer = gather(shares(outer), BAND)
    received = swap(
        lax.dynamic_slice_in_dim(orbitals, core * (rows - edge), edge, 0),
        lax.dynamic_slice_in_dim(orbitals, (1 - core) * (rows - edge), edge, 0),
    )
    ham_inner = gather(shares(inner, *received), BAND)
    first_outer, *faces = run(
        functools.partial(outer_kernel, outer),
        [(len(outer) * tile, width), face, face],
        (ham_outer, orbitals, *received),
    )
    first, second, *faces = run(
        functools.partial(second_kernel, outer, inner),
        [whole, whole, face, face],
        (ham_outer, ham_inner, orbitals, first_outer, *swap(*faces)),
    )
    third, copies, *faces = run(
        functools.partial(third_kernel, outer, inner),
        [whole, (ny, rows, width), face, face],
        (ham_outer, ham_inner, second, first, *swap(*faces)),
        (pltpu.SemaphoreType.DMA((ny,)),),
        far_outs=(1,),
    )
    third_all = gather(copies, "y")
    (applied,) = run(
        functools.partial(applied_kernel, outer, inner),
        [whole],
        (ham_outer, ham_inner, third, *swap(*faces)),
    )
    other = lax.ppermute(applied, "xl", [(0, 1), (1, 0)])

    rows_all = rows * lax.axis_size(SLAB)
    scale = 1.0 / math.sqrt(float(rows_all) * float(width * nband))
    share = ny * width // near

    (partial_gram,) = call(gram_kernel, [(near, share, 2 * width)], (third_all, applied, other))
    (summed,) = call(
        functools.partial(sum_kernel, None),
        [(far, share, 2 * width)],
        (gather(partial_gram, NEAR),),
    )
    (scaled,) = call(
        functools.partial(sum_kernel, scale),
        [(near, share, 2 * width)],
        (gather(summed, "z2"),),
    )
    gram = gather(scaled, NEAR)
    (partial_out,) = call(
        mixed_kernel, [(nband, rows // nband, 2 * width)], (third_all, gram, applied)
    )
    (out,) = call(
        final_kernel, [(rows // nband, nband * width)], (gather(partial_out, BAND),), last=True
    )
    return out


def solution(mesh):
    slabs = mesh.shape["slab"]
    fine = Mesh(
        np.asarray(mesh.devices).reshape(slabs // 16, 4, 2, 2, mesh.shape["band"] // 2, 2),
        SLAB + BAND,
    )
    in_specs = (P(SLAB, None, BAND, None), P(SLAB, None), P(SLAB, BAND))
    out_specs = P(SLAB + BAND, None)
    return jax.shard_map(body, mesh=fine, in_specs=in_specs, out_specs=out_specs, check_vma=False)
```

```python
import functools
import math

import jax
import jax.numpy as jnp
import numpy as np
from jax import lax
from jax.experimental import pallas as pl
from jax.experimental.pallas import tpu as pltpu
from jax.sharding import Mesh
from jax.sharding import PartitionSpec as P

SLAB = ("z2", "z1", "xh", "core")
BAND = ("y", "xl")
NEAR = ("z1", "xh")
PAIR = [(0, 1), (1, 0)]
FACE = 2
F32 = jnp.float32
BF16 = jnp.bfloat16

VMEM = pl.BlockSpec(memory_space=pltpu.VMEM)
SMEM = pl.BlockSpec(memory_space=pltpu.SMEM)
HBM = pl.BlockSpec(memory_space=pltpu.MemorySpace.HBM)


def dot(a, b, dims=((1,), (0,))):
    return lax.dot_general(a, b, (dims, ((), ())), preferred_element_type=F32)


def call(kernel, outs, args, scratch=(), smem=0, far=None, far_outs=(), last=False):
    far = far or {}
    args = [
        x if i < smem or i in far else pltpu.with_memory_space_constraint(x, pltpu.VMEM)
        for i, x in enumerate(args)
    ]
    shapes = []
    for i, out in enumerate(outs):
        make = jax.ShapeDtypeStruct if last or i in far_outs else pltpu.VMEM
        shapes.append(make(out, BF16) if isinstance(out, tuple) else out)
    return pl.pallas_call(
        kernel,
        out_shape=shapes,
        in_specs=[
            SMEM if i < smem else HBM if far.get(i, False) else VMEM for i in range(len(args))
        ],
        out_specs=[HBM if i in far_outs else VMEM for i in range(len(outs))],
        scratch_shapes=list(scratch),
    )(*args)


def combine_kernel(nbr, ham, out):
    blocks, slots = ham.shape[0], ham.shape[1]
    width = ham.shape[3]
    for r in range(blocks):
        layer = FACE + r // FACE * FACE
        for k, position in enumerate((r, layer, layer + 1, r + 2 * FACE)):
            total = jnp.zeros(ham.shape[2:], F32)
            for j in range(slots):
                keep = (nbr[r, j] == position).astype(F32)
                total = total + keep * ham[r, j].astype(F32)
            total = total.astype(BF16)
            for copy in range(out.shape[0]):
                out[copy, r, :, k * width : (k + 1) * width] = total


def product(ham, r, ext):
    tile = ham.shape[3] // 4
    layer = FACE + r // FACE * FACE
    rhs = jnp.concatenate(
        [
            ext[r * tile : (r + 1) * tile],
            ext[layer * tile : (layer + FACE) * tile],
            ext[(r + 2 * FACE) * tile : (r + 2 * FACE + 1) * tile],
        ],
        axis=0,
    )
    return dot(ham[:, r].reshape(tile, 4 * tile), rhs)


def fill(core, ext, vec, from_far, from_near):
    edge, rows = from_far.shape[0], vec.shape[0]
    c = core[0]
    ext[edge : edge + rows] = vec[...]
    ext[pl.ds(pl.multiple_of(c * (edge + rows), edge), edge)] = from_far[...]
    ext[pl.ds(pl.multiple_of((1 - c) * (edge + rows), edge), edge)] = from_near[...]


def step_kernel(prior, core, ham, vec, from_far, from_near, *rest):
    before = rest[0] if prior else None
    out, far, near, ext, *copying = rest[1:] if prior else rest
    if copying:
        out, copies, far, near, ext, sems = rest[1:]
    edge, rows = far.shape[0], vec.shape[0]
    tile = edge // FACE
    fill(core, ext, vec, from_far, from_near)
    for r in range(rows // tile):
        here = slice(r * tile, (r + 1) * tile)
        value = product(ham, r, ext)
        if prior:
            value = 2.0 * value - before[here].astype(F32)
        out[here] = value.astype(BF16)
    sends = []
    if copying:
        for i in range(copies.shape[0]):
            sends.append(pltpu.make_async_copy(out, copies.at[i], sems.at[i]))
    for send in sends:
        send.start()
    c = core[0]
    far[...] = out[pl.ds(pl.multiple_of(c * (rows - edge), edge), edge)]
    near[...] = out[pl.ds(pl.multiple_of((1 - c) * (rows - edge), edge), edge)]
    for send in sends:
        send.wait()


def inner_kernel(ham, vec, out, ext):
    rows = vec.shape[0]
    edge = (ext.shape[0] - rows) // 2
    tile = edge // FACE
    ext[edge : edge + rows] = vec[...]
    for i in range(out.shape[0] // tile):
        out[i * tile : (i + 1) * tile] = product(ham, FACE + i, ext).astype(BF16)


def outer_kernel(core, ham, vec, from_far, from_near, out, ext):
    edge, rows = from_far.shape[0], vec.shape[0]
    tile = edge // FACE
    fill(core, ext, vec, from_far, from_near)
    for i, r in enumerate((*range(FACE), *range(rows // tile - FACE, rows // tile))):
        out[i * tile : (i + 1) * tile] = product(ham, r, ext).astype(BF16)


def gram_kernel(core, third_far, inner, outer, inner2, outer2, third, give, mine, sems):
    rows, width = third.shape[1], third.shape[2]
    edge = outer.shape[0] // 2
    count = third.shape[0]
    fetches = [
        pltpu.make_async_copy(third_far.at[y], third.at[y], sems.at[y]) for y in range(count)
    ]
    for fetch in fetches:
        fetch.start()
    own = jnp.concatenate([outer[:edge], inner[...], outer[edge:]], axis=0)
    other = jnp.concatenate([outer2[:edge], inner2[...], outer2[edge:]], axis=0)
    right = jnp.concatenate([own, other], axis=1)
    for fetch in fetches:
        fetch.wait()
    half = count // 2
    c = core[0]
    for y in range(half):
        here = slice(y * width, (y + 1) * width)
        give[here] = dot(third[(1 - c) * half + y], right, ((0,), (0,))).astype(BF16)
        mine[here] = dot(third[c * half + y], right, ((0,), (0,)))


def join_kernel(mine, received, out):
    share = out.shape[1]
    total = (mine[...] + received[...].astype(F32)).astype(BF16)
    for i in range(out.shape[0]):
        out[i] = total[i * share : (i + 1) * share]


def sum_kernel(scale, parts, out):
    total = parts[0].astype(F32)
    for i in range(1, parts.shape[0]):
        total = total + parts[i].astype(F32)
    if scale is not None:
        total = total * scale
    total = total.astype(BF16)
    for copy in range(out.shape[0]):
        out[copy] = total


def mixed_kernel(core, third, gram, gram2, inner, outer, out):
    strips, height, width = out.shape[0], out.shape[1], third.shape[2]
    half = third.shape[0] // 2
    edge = outer.shape[0] // (2 * height)
    c = core[0]
    weights = jnp.concatenate(
        [g[...].reshape(half * width, g.shape[2]) for g in (gram, gram2)], axis=0
    )
    for s in range(strips):
        here = slice(s * height, (s + 1) * height)
        order = [c * half + y for y in range(half)] + [(1 - c) * half + y for y in range(half)]
        left = jnp.concatenate([third[y, here] for y in order], axis=1)
        value = dot(left, weights)
        if s < edge:
            applied = outer[here]
        elif s < strips - edge:
            applied = inner[(s - edge) * height : (s - edge + 1) * height]
        else:
            at = (s - strips + 2 * edge) * height
            applied = outer[at : at + height]
        out[s, :, :width] = (applied.astype(F32) - value[:, :width]).astype(BF16)
        out[s, :, width:] = (-value[:, width:]).astype(BF16)


def final_kernel(parts, out):
    width = parts.shape[2] // 2
    for b in range(parts.shape[0]):
        value = parts[b, :, :width].astype(F32) + parts[b ^ 1, :, width:].astype(F32)
        out[:, b * width : (b + 1) * width] = value.astype(BF16)


def gather(copies, axes):
    return lax.all_to_all(copies, axes, 0, 0, tiled=True)


def swap(far, near):
    count = lax.axis_size(SLAB)
    pairs = [(s, (s + 1) % count if s % 2 else (s - 1) % count) for s in range(count)]
    from_far = lax.ppermute(far, SLAB, pairs)
    return from_far, lax.ppermute(near, "core", PAIR)


def body(hamiltonian, neighbors, orbitals):
    blocks, _, strip, tile = hamiltonian.shape
    rows, width = orbitals.shape
    edge = FACE * tile
    ny, nband, near, far = (lax.axis_size(a) for a in ("y", BAND, NEAR, "z2"))
    core = lax.axis_index("core")
    scalar = core.astype(jnp.int32).reshape(1)

    (shares,) = call(
        combine_kernel, [(nband, blocks, strip, 4 * tile)], (neighbors, hamiltonian), smem=1, far={1: False}
    )
    tiles = gather(shares, BAND)
    received = swap(
        lax.dynamic_slice_in_dim(orbitals, core * (rows - edge), edge, 0),
        lax.dynamic_slice_in_dim(orbitals, (1 - core) * (rows - edge), edge, 0),
    )

    ext = pltpu.VMEM((rows + 2 * edge, width), BF16)
    whole, face, part = (rows, width), (edge, width), (rows - 2 * edge, width)

    def step(vec, received, before=()):
        return call(
            functools.partial(step_kernel, bool(before)),
            [whole, face, face],
            (scalar, tiles, vec, *received, *before),
            (ext,),
            smem=1,
        )

    first, *faces = step(orbitals, received)
    second, *faces = step(first, swap(*faces), (orbitals,))
    third, copies, *faces = call(
        functools.partial(step_kernel, True),
        [whole, (ny, rows, width), face, face],
        (scalar, tiles, second, *swap(*faces), first),
        (ext, pltpu.SemaphoreType.DMA((ny,))),
        smem=1,
        far_outs=(1,),
    )
    received = swap(*faces)
    third_far = gather(copies, "y")
    (inner,) = call(inner_kernel, [part], (tiles, third), (ext,))
    inner2 = lax.ppermute(inner, "xl", PAIR)
    (outer,) = call(outer_kernel, [(2 * edge, width)], (scalar, tiles, third, *received), (ext,), smem=1)
    outer2 = lax.ppermute(outer, "xl", PAIR)

    rows_all = rows * lax.axis_size(SLAB)
    scale = 1.0 / math.sqrt(float(rows_all) * float(width * nband))
    depth, columns = ny * width // 2, 2 * width
    share = depth // near
    third_all, give, mine = call(
        gram_kernel,
        [(ny, rows, width), (depth, columns), pltpu.VMEM((depth, columns), F32)],
        (scalar, third_far, inner, outer, inner2, outer2),
        (pltpu.SemaphoreType.DMA((ny,)),),
        smem=1,
        far={1: True},
    )
    received = lax.ppermute(give, "core", PAIR)
    (joined,) = call(join_kernel, [(near, share, columns)], (mine, received))
    (summed,) = call(
        functools.partial(sum_kernel, None), [(far, share, columns)], (gather(joined, NEAR),)
    )
    (scaled,) = call(
        functools.partial(sum_kernel, scale), [(near, share, columns)], (gather(summed, "z2"),)
    )
    gram = gather(scaled, NEAR)
    gram2 = lax.ppermute(gram, "core", PAIR)
    (partial_out,) = call(
        mixed_kernel,
        [(nband, rows // nband, columns)],
        (scalar, third_all, gram, gram2, inner, outer),
        smem=1,
    )
    (out,) = call(
        final_kernel, [(rows // nband, nband * width)], (gather(partial_out, BAND),), last=True
    )
    return out


def solution(mesh):
    slabs = mesh.shape["slab"]
    fine = Mesh(
        np.asarray(mesh.devices).reshape(slabs // 16, 4, 2, 2, mesh.shape["band"] // 2, 2),
        SLAB + BAND,
    )
    in_specs = (P(SLAB, None, BAND, None), P(SLAB, None), P(SLAB, BAND))
    out_specs = P(SLAB + BAND, None)
    return jax.shard_map(body, mesh=fine, in_specs=in_specs, out_specs=out_specs, check_vma=False)
```

```python
import functools
import math

import jax
import jax.numpy as jnp
import numpy as np
from jax import lax
from jax.experimental import pallas as pl
from jax.experimental.pallas import tpu as pltpu
from jax.sharding import Mesh
from jax.sharding import PartitionSpec as P

SLAB = ("z2", "z1", "xh", "core")
BAND = ("y", "xl")
NEAR = ("z1", "xh")
PAIR = [(0, 1), (1, 0)]
FACE = 2
F32 = jnp.float32
BF16 = jnp.bfloat16

VMEM = pl.BlockSpec(memory_space=pltpu.VMEM)
SMEM = pl.BlockSpec(memory_space=pltpu.SMEM)
FAR = pltpu.MemorySpace.HBM
HBM = pl.BlockSpec(memory_space=FAR)


def dot(a, b, dims=((1,), (0,))):
    return lax.dot_general(a, b, (dims, ((), ())), preferred_element_type=F32)


def call(kernel, outs, args, scratch=(), smem=0, far=None, far_outs=(), last=False):
    far = far or {}
    args = [
        x if i < smem
        else pltpu.with_memory_space_constraint(x, FAR if far.get(i, False) else pltpu.VMEM)
        for i, x in enumerate(args)
    ]
    shapes = []
    for i, out in enumerate(outs):
        make = jax.ShapeDtypeStruct if last or i in far_outs else pltpu.VMEM
        shapes.append(make(out, BF16) if isinstance(out, tuple) else out)
    return pl.pallas_call(
        kernel,
        out_shape=shapes,
        in_specs=[
            SMEM if i < smem else HBM if far.get(i, False) else VMEM for i in range(len(args))
        ],
        out_specs=[HBM if i in far_outs else VMEM for i in range(len(outs))],
        scratch_shapes=list(scratch),
    )(*args)


def combine_kernel(nbr_far, ham_far, out, nbr, ham, sems):
    fetches = [
        pltpu.make_async_copy(nbr_far, nbr, sems.at[0]),
        pltpu.make_async_copy(ham_far, ham, sems.at[1]),
    ]
    for fetch in fetches:
        fetch.start()
    for fetch in fetches:
        fetch.wait()
    blocks, slots = ham.shape[0], ham.shape[1]
    width = ham.shape[3]
    for r in range(blocks):
        layer = FACE + r // FACE * FACE
        for k, position in enumerate((r, layer, layer + 1, r + 2 * FACE)):
            total = jnp.zeros(ham.shape[2:], F32)
            for j in range(slots):
                keep = (nbr[r, j] == position).astype(F32)
                total = total + keep * ham[r, j].astype(F32)
            total = total.astype(BF16)
            for copy in range(out.shape[0]):
                out[copy, r, :, k * width : (k + 1) * width] = total


def product(ham, r, ext):
    tile = ham.shape[3] // 4
    layer = FACE + r // FACE * FACE
    rhs = jnp.concatenate(
        [
            ext[r * tile : (r + 1) * tile],
            ext[layer * tile : (layer + FACE) * tile],
            ext[(r + 2 * FACE) * tile : (r + 2 * FACE + 1) * tile],
        ],
        axis=0,
    )
    return dot(ham[:, r].reshape(tile, 4 * tile), rhs)


def fill(core, ext, vec, from_far, from_near):
    edge, rows = from_far.shape[0], vec.shape[0]
    c = core[0]
    ext[edge : edge + rows] = vec[...]
    ext[pl.ds(pl.multiple_of(c * (edge + rows), edge), edge)] = from_far[...]
    ext[pl.ds(pl.multiple_of((1 - c) * (edge + rows), edge), edge)] = from_near[...]


def step_kernel(prior, core, ham, vec, from_far, from_near, *rest):
    before = rest[0] if prior else None
    out, far, near, ext, *copying = rest[1:] if prior else rest
    if copying:
        out, copies, far, near, ext, sems = rest[1:]
    edge, rows = far.shape[0], vec.shape[0]
    tile = edge // FACE
    fill(core, ext, vec, from_far, from_near)
    for r in range(rows // tile):
        here = slice(r * tile, (r + 1) * tile)
        value = product(ham, r, ext)
        if prior:
            value = 2.0 * value - before[here].astype(F32)
        out[here] = value.astype(BF16)
    sends = []
    if copying:
        for i in range(copies.shape[0]):
            sends.append(pltpu.make_async_copy(out, copies.at[i], sems.at[i]))
    for send in sends:
        send.start()
    c = core[0]
    far[...] = out[pl.ds(pl.multiple_of(c * (rows - edge), edge), edge)]
    near[...] = out[pl.ds(pl.multiple_of((1 - c) * (rows - edge), edge), edge)]
    for send in sends:
        send.wait()


def inner_kernel(ham, vec, out, ext):
    rows = vec.shape[0]
    edge = (ext.shape[0] - rows) // 2
    tile = edge // FACE
    ext[edge : edge + rows] = vec[...]
    for i in range(out.shape[0] // tile):
        out[i * tile : (i + 1) * tile] = product(ham, FACE + i, ext).astype(BF16)


def outer_kernel(core, ham, vec, from_far, from_near, out, ext):
    edge, rows = from_far.shape[0], vec.shape[0]
    tile = edge // FACE
    fill(core, ext, vec, from_far, from_near)
    for i, r in enumerate((*range(FACE), *range(rows // tile - FACE, rows // tile))):
        out[i * tile : (i + 1) * tile] = product(ham, r, ext).astype(BF16)


def fetch_kernel(far, out, sem):
    fetch = pltpu.make_async_copy(far, out, sem.at[0])
    fetch.start()
    fetch.wait()


def gram_kernel(side, core, third, inner, outer, inner2, outer2, out):
    width, half = third.shape[2], third.shape[0] // 2
    edge = outer.shape[0] // 2
    start = (core[0] if side == 0 else 1 - core[0]) * half
    own = jnp.concatenate([outer[:edge], inner[...], outer[edge:]], axis=0)
    other = jnp.concatenate([outer2[:edge], inner2[...], outer2[edge:]], axis=0)
    right = jnp.concatenate([own, other], axis=1)
    for y in range(half):
        block = dot(third[start + y], right, ((0,), (0,)))
        out[y * width : (y + 1) * width] = block.astype(out.dtype)


def join_kernel(mine, received, out):
    share = out.shape[1]
    total = (mine[...] + received[...].astype(F32)).astype(BF16)
    for i in range(out.shape[0]):
        out[i] = total[i * share : (i + 1) * share]


def sum_kernel(scale, parts, out):
    total = parts[0].astype(F32)
    for i in range(1, parts.shape[0]):
        total = total + parts[i].astype(F32)
    if scale is not None:
        total = total * scale
    total = total.astype(BF16)
    for copy in range(out.shape[0]):
        out[copy] = total


def mixed_kernel(core, third, gram, gram2, inner, outer, out):
    strips, height, width = out.shape[0], out.shape[1], third.shape[2]
    half = third.shape[0] // 2
    edge = outer.shape[0] // (2 * height)
    c = core[0]
    weights = jnp.concatenate(
        [g[...].reshape(half * width, g.shape[2]) for g in (gram, gram2)], axis=0
    )
    for s in range(strips):
        here = slice(s * height, (s + 1) * height)
        order = [c * half + y for y in range(half)] + [(1 - c) * half + y for y in range(half)]
        left = jnp.concatenate([third[y, here] for y in order], axis=1)
        value = dot(left, weights)
        if s < edge:
            applied = outer[here]
        elif s < strips - edge:
            applied = inner[(s - edge) * height : (s - edge + 1) * height]
        else:
            at = (s - strips + 2 * edge) * height
            applied = outer[at : at + height]
        out[s, :, :width] = (applied.astype(F32) - value[:, :width]).astype(BF16)
        out[s, :, width:] = (-value[:, width:]).astype(BF16)


def final_kernel(parts, out):
    width = parts.shape[2] // 2
    for b in range(parts.shape[0]):
        value = parts[b, :, :width].astype(F32) + parts[b ^ 1, :, width:].astype(F32)
        out[:, b * width : (b + 1) * width] = value.astype(BF16)


def gather(copies, axes):
    return lax.all_to_all(copies, axes, 0, 0, tiled=True)


def swap(far, near):
    count = lax.axis_size(SLAB)
    pairs = [(s, (s + 1) % count if s % 2 else (s - 1) % count) for s in range(count)]
    from_far = lax.ppermute(far, SLAB, pairs)
    return from_far, lax.ppermute(near, "core", PAIR)


def filtered(hamiltonian, neighbors, orbitals):
    blocks, _, strip, tile = hamiltonian.shape
    rows, width = orbitals.shape
    edge = FACE * tile
    ny, nband, near, far = (lax.axis_size(a) for a in ("y", BAND, NEAR, "z2"))
    core = lax.axis_index("core")
    scalar = core.astype(jnp.int32).reshape(1)

    (shares,) = call(
        combine_kernel,
        [(nband, blocks, strip, 4 * tile)],
        (neighbors, hamiltonian),
        (
            pltpu.SMEM(neighbors.shape, neighbors.dtype),
            pltpu.VMEM(hamiltonian.shape, BF16),
            pltpu.SemaphoreType.DMA((2,)),
        ),
        far={0: True, 1: True},
    )
    tiles = gather(shares, BAND)
    received = swap(
        lax.dynamic_slice_in_dim(orbitals, core * (rows - edge), edge, 0),
        lax.dynamic_slice_in_dim(orbitals, (1 - core) * (rows - edge), edge, 0),
    )

    ext = pltpu.VMEM((rows + 2 * edge, width), BF16)
    whole, face, part = (rows, width), (edge, width), (rows - 2 * edge, width)

    def step(vec, received, before=()):
        return call(
            functools.partial(step_kernel, bool(before)),
            [whole, face, face],
            (scalar, tiles, vec, *received, *before),
            (ext,),
            smem=1,
        )

    first, *faces = step(orbitals, received)
    second, *faces = step(first, swap(*faces), (orbitals,))
    third, copies, *faces = call(
        functools.partial(step_kernel, True),
        [whole, (ny, rows, width), face, face],
        (scalar, tiles, second, *swap(*faces), first),
        (ext, pltpu.SemaphoreType.DMA((ny,))),
        smem=1,
        far_outs=(1,),
    )
    received = swap(*faces)
    third_far = gather(copies, "y")
    (inner,) = call(inner_kernel, [part], (tiles, third), (ext,))
    inner2 = lax.ppermute(inner, "xl", PAIR)
    (outer,) = call(outer_kernel, [(2 * edge, width)], (scalar, tiles, third, *received), (ext,), smem=1)
    outer2 = lax.ppermute(outer, "xl", PAIR)
    (third_all,) = call(
        fetch_kernel,
        [(ny, rows, width)],
        (third_far,),
        (pltpu.SemaphoreType.DMA((1,)),),
        far={0: True},
    )

    rows_all = rows * lax.axis_size(SLAB)
    scale = 1.0 / math.sqrt(float(rows_all) * float(width * nband))
    depth, columns = ny * width // 2, 2 * width
    share = depth // near

    def gram_half(side, dtype):
        (out,) = call(
            functools.partial(gram_kernel, side),
            [pltpu.VMEM((depth, columns), dtype)],
            (scalar, third_all, inner, outer, inner2, outer2),
            smem=1,
        )
        return out

    received = lax.ppermute(gram_half(1, BF16), "core", PAIR)
    mine = gram_half(0, F32)
    (joined,) = call(join_kernel, [(near, share, columns)], (mine, received))
    (summed,) = call(
        functools.partial(sum_kernel, None), [(far, share, columns)], (gather(joined, NEAR),)
    )
    (scaled,) = call(
        functools.partial(sum_kernel, scale), [(near, share, columns)], (gather(summed, "z2"),)
    )
    gram = gather(scaled, NEAR)
    gram2 = lax.ppermute(gram, "core", PAIR)
    (partial_out,) = call(
        mixed_kernel,
        [(nband, rows // nband, columns)],
        (scalar, third_all, gram, gram2, inner, outer),
        smem=1,
    )
    (out,) = call(
        final_kernel, [(rows // nband, nband * width)], (gather(partial_out, BAND),), last=True
    )
    return out


def solution(mesh):
    slabs = mesh.shape["slab"]
    fine = Mesh(
        np.asarray(mesh.devices).reshape(slabs // 16, 4, 2, 2, mesh.shape["band"] // 2, 2),
        SLAB + BAND,
    )
    in_specs = (P(SLAB, None, BAND, None), P(SLAB, None), P(SLAB, BAND))
    out_specs = P(SLAB + BAND, None)
    return jax.shard_map(filtered, mesh=fine, in_specs=in_specs, out_specs=out_specs, check_vma=False)
```

```python
import functools
import math

import jax
import jax.numpy as jnp
import numpy as np
from jax import lax
from jax.experimental import pallas as pl
from jax.experimental.pallas import tpu as pltpu
from jax.sharding import Mesh
from jax.sharding import PartitionSpec as P

SLAB = ("z2", "z1", "xh", "core")
BAND = ("y", "xl")
NEAR = ("z1", "xh", "core")
PAIR = [(0, 1), (1, 0)]
FACE = 2
F32 = jnp.float32
BF16 = jnp.bfloat16

VMEM = pl.BlockSpec(memory_space=pltpu.VMEM)
SMEM = pl.BlockSpec(memory_space=pltpu.SMEM)
FAR = pltpu.MemorySpace.HBM
HBM = pl.BlockSpec(memory_space=FAR)


def dot(a, b, dims=((1,), (0,))):
    return lax.dot_general(a, b, (dims, ((), ())), preferred_element_type=F32)


def call(kernel, outs, args, scratch=(), smem=0, far=None, far_outs=(), last=False):
    far = far or {}
    args = [
        x if i < smem
        else pltpu.with_memory_space_constraint(x, FAR if far.get(i, False) else pltpu.VMEM)
        for i, x in enumerate(args)
    ]
    shapes = []
    for i, out in enumerate(outs):
        make = jax.ShapeDtypeStruct if last or i in far_outs else pltpu.VMEM
        shapes.append(make(out, BF16) if isinstance(out, tuple) else out)
    return pl.pallas_call(
        kernel,
        out_shape=shapes,
        in_specs=[
            SMEM if i < smem else HBM if far.get(i, False) else VMEM for i in range(len(args))
        ],
        out_specs=[HBM if i in far_outs else VMEM for i in range(len(outs))],
        scratch_shapes=list(scratch),
    )(*args)


def combine_kernel(nbr_far, ham_far, out, nbr, ham, sems):
    fetches = [
        pltpu.make_async_copy(nbr_far, nbr, sems.at[0]),
        pltpu.make_async_copy(ham_far, ham, sems.at[1]),
    ]
    for fetch in fetches:
        fetch.start()
    for fetch in fetches:
        fetch.wait()
    blocks, slots = ham.shape[0], ham.shape[1]
    width = ham.shape[3]
    for r in range(blocks):
        layer = FACE + r // FACE * FACE
        for k, position in enumerate((r, layer, layer + 1, r + 2 * FACE)):
            total = jnp.zeros(ham.shape[2:], F32)
            for j in range(slots):
                keep = (nbr[r, j] == position).astype(F32)
                total = total + keep * ham[r, j].astype(F32)
            total = total.astype(BF16)
            for copy in range(out.shape[0]):
                out[copy, r, :, k * width : (k + 1) * width] = total


def product(ham, r, ext):
    tile = ham.shape[3] // 4
    layer = FACE + r // FACE * FACE
    rhs = jnp.concatenate(
        [
            ext[r * tile : (r + 1) * tile],
            ext[layer * tile : (layer + FACE) * tile],
            ext[(r + 2 * FACE) * tile : (r + 2 * FACE + 1) * tile],
        ],
        axis=0,
    )
    return dot(ham[:, r].reshape(tile, 4 * tile), rhs)


def fill(core, ext, vec, from_far, from_near):
    edge, rows = from_far.shape[0], vec.shape[0]
    c = core[0]
    ext[edge : edge + rows] = vec[...]
    ext[pl.ds(pl.multiple_of(c * (edge + rows), edge), edge)] = from_far[...]
    ext[pl.ds(pl.multiple_of((1 - c) * (edge + rows), edge), edge)] = from_near[...]


def step_kernel(prior, core, ham, vec, from_far, from_near, *rest):
    before = rest[0] if prior else None
    out, far, near, ext, *copying = rest[1:] if prior else rest
    if copying:
        out, copies, far, near, ext, sems = rest[1:]
    edge, rows = far.shape[0], vec.shape[0]
    tile = edge // FACE
    fill(core, ext, vec, from_far, from_near)
    for r in range(rows // tile):
        here = slice(r * tile, (r + 1) * tile)
        value = product(ham, r, ext)
        if prior:
            value = 2.0 * value - before[here].astype(F32)
        out[here] = value.astype(BF16)
    sends = []
    if copying:
        for i in range(copies.shape[0]):
            sends.append(pltpu.make_async_copy(out, copies.at[i], sems.at[i]))
    for send in sends:
        send.start()
    c = core[0]
    far[...] = out[pl.ds(pl.multiple_of(c * (rows - edge), edge), edge)]
    near[...] = out[pl.ds(pl.multiple_of((1 - c) * (rows - edge), edge), edge)]
    for send in sends:
        send.wait()


def inner_kernel(ham, vec, out, ext):
    rows = vec.shape[0]
    edge = (ext.shape[0] - rows) // 2
    tile = edge // FACE
    ext[edge : edge + rows] = vec[...]
    for i in range(out.shape[0] // tile):
        out[i * tile : (i + 1) * tile] = product(ham, FACE + i, ext).astype(BF16)


def outer_kernel(core, ham, vec, from_far, from_near, out, ext):
    edge, rows = from_far.shape[0], vec.shape[0]
    tile = edge // FACE
    fill(core, ext, vec, from_far, from_near)
    for i, r in enumerate((*range(FACE), *range(rows // tile - FACE, rows // tile))):
        out[i * tile : (i + 1) * tile] = product(ham, r, ext).astype(BF16)


def fetch_kernel(far, out, sem):
    fetch = pltpu.make_async_copy(far, out, sem.at[0])
    fetch.start()
    fetch.wait()


def gram_kernel(third, inner, outer, inner2, outer2, out):
    share, width = out.shape[1], third.shape[2]
    per = width // share
    edge = outer.shape[0] // 2
    own = jnp.concatenate([outer[:edge], inner[...], outer[edge:]], axis=0)
    other = jnp.concatenate([outer2[:edge], inner2[...], outer2[edge:]], axis=0)
    right = jnp.concatenate([own, other], axis=1)
    for y in range(third.shape[0]):
        block = dot(third[y], right, ((0,), (0,))).astype(BF16)
        for i in range(per):
            out[y * per + i] = block[i * share : (i + 1) * share]


def sum_kernel(scale, parts, out):
    total = parts[0].astype(F32)
    for i in range(1, parts.shape[0]):
        total = total + parts[i].astype(F32)
    if scale is not None:
        total = total * scale
    total = total.astype(BF16)
    for copy in range(out.shape[0]):
        out[copy] = total


def mixed_kernel(third, gram, inner, outer, out):
    strips, height, width = out.shape[0], out.shape[1], third.shape[2]
    count = third.shape[0]
    edge = outer.shape[0] // (2 * height)
    weights = gram[...].reshape(count * width, gram.shape[2])
    for s in range(strips):
        here = slice(s * height, (s + 1) * height)
        left = jnp.concatenate([third[y, here] for y in range(count)], axis=1)
        value = dot(left, weights)
        if s < edge:
            applied = outer[here]
        elif s < strips - edge:
            applied = inner[(s - edge) * height : (s - edge + 1) * height]
        else:
            at = (s - strips + 2 * edge) * height
            applied = outer[at : at + height]
        out[s, :, :width] = (applied.astype(F32) - value[:, :width]).astype(BF16)
        out[s, :, width:] = (-value[:, width:]).astype(BF16)


def final_kernel(parts, out):
    width = parts.shape[2] // 2
    for b in range(parts.shape[0]):
        value = parts[b, :, :width].astype(F32) + parts[b ^ 1, :, width:].astype(F32)
        out[:, b * width : (b + 1) * width] = value.astype(BF16)


def gather(copies, axes):
    return lax.all_to_all(copies, axes, 0, 0, tiled=True)


def swap(far, near):
    count = lax.axis_size(SLAB)
    pairs = [(s, (s + 1) % count if s % 2 else (s - 1) % count) for s in range(count)]
    from_far = lax.ppermute(far, SLAB, pairs)
    return from_far, lax.ppermute(near, "core", PAIR)


def filtered(hamiltonian, neighbors, orbitals):
    blocks, _, strip, tile = hamiltonian.shape
    rows, width = orbitals.shape
    edge = FACE * tile
    ny, nband, near, far = (lax.axis_size(a) for a in ("y", BAND, NEAR, "z2"))
    core = lax.axis_index("core")
    scalar = core.astype(jnp.int32).reshape(1)

    (shares,) = call(
        combine_kernel,
        [(nband, blocks, strip, 4 * tile)],
        (neighbors, hamiltonian),
        (
            pltpu.SMEM(neighbors.shape, neighbors.dtype),
            pltpu.VMEM(hamiltonian.shape, BF16),
            pltpu.SemaphoreType.DMA((2,)),
        ),
        far={0: True, 1: True},
    )
    tiles = gather(shares, BAND)
    received = swap(
        lax.dynamic_slice_in_dim(orbitals, core * (rows - edge), edge, 0),
        lax.dynamic_slice_in_dim(orbitals, (1 - core) * (rows - edge), edge, 0),
    )

    ext = pltpu.VMEM((rows + 2 * edge, width), BF16)
    whole, face, part = (rows, width), (edge, width), (rows - 2 * edge, width)

    def step(vec, received, before=()):
        return call(
            functools.partial(step_kernel, bool(before)),
            [whole, face, face],
            (scalar, tiles, vec, *received, *before),
            (ext,),
            smem=1,
        )

    first, *faces = step(orbitals, received)
    second, *faces = step(first, swap(*faces), (orbitals,))
    third, copies, *faces = call(
        functools.partial(step_kernel, True),
        [whole, (ny, rows, width), face, face],
        (scalar, tiles, second, *swap(*faces), first),
        (ext, pltpu.SemaphoreType.DMA((ny,))),
        smem=1,
        far_outs=(1,),
    )
    received = swap(*faces)
    third_far = gather(copies, "y")
    (inner,) = call(inner_kernel, [part], (tiles, third), (ext,))
    inner2 = lax.ppermute(inner, "xl", PAIR)
    (outer,) = call(outer_kernel, [(2 * edge, width)], (scalar, tiles, third, *received), (ext,), smem=1)
    outer2 = lax.ppermute(outer, "xl", PAIR)
    (third_all,) = call(
        fetch_kernel,
        [(ny, rows, width)],
        (third_far,),
        (pltpu.SemaphoreType.DMA((1,)),),
        far={0: True},
    )

    rows_all = rows * lax.axis_size(SLAB)
    scale = 1.0 / math.sqrt(float(rows_all) * float(width * nband))
    columns = 2 * width
    share = ny * width // near
    (partial_gram,) = call(
        gram_kernel, [(near, share, columns)], (third_all, inner, outer, inner2, outer2)
    )
    (summed,) = call(
        functools.partial(sum_kernel, None), [(far, share, columns)], (gather(partial_gram, NEAR),)
    )
    (scaled,) = call(
        functools.partial(sum_kernel, scale), [(near, share, columns)], (gather(summed, "z2"),)
    )
    gram = gather(scaled, NEAR)
    (partial_out,) = call(
        mixed_kernel,
        [(nband, rows // nband, columns)],
        (third_all, gram, inner, outer),
    )
    (out,) = call(
        final_kernel, [(rows // nband, nband * width)], (gather(partial_out, BAND),), last=True
    )
    return out


def solution(mesh):
    slabs = mesh.shape["slab"]
    fine = Mesh(
        np.asarray(mesh.devices).reshape(slabs // 16, 4, 2, 2, mesh.shape["band"] // 2, 2),
        SLAB + BAND,
    )
    in_specs = (P(SLAB, None, BAND, None), P(SLAB, None), P(SLAB, BAND))
    out_specs = P(SLAB + BAND, None)
    return jax.shard_map(filtered, mesh=fine, in_specs=in_specs, out_specs=out_specs, check_vma=False)
```

```python
import functools
import math

import jax
import jax.numpy as jnp
import numpy as np
from jax import lax
from jax.experimental import pallas as pl
from jax.experimental.pallas import tpu as pltpu
from jax.sharding import Mesh
from jax.sharding import PartitionSpec as P

SLAB = ("z2", "z1", "xh", "core")
BAND = ("y", "xl")
NEAR = ("z1", "core")
FURTHER = ("z2", "xh")
PAIR = [(0, 1), (1, 0)]
FACE = 2
F32 = jnp.float32
BF16 = jnp.bfloat16

VMEM = pl.BlockSpec(memory_space=pltpu.VMEM)
SMEM = pl.BlockSpec(memory_space=pltpu.SMEM)
FAR = pltpu.MemorySpace.HBM
HBM = pl.BlockSpec(memory_space=FAR)


def dot(a, b, dims=((1,), (0,))):
    return lax.dot_general(a, b, (dims, ((), ())), preferred_element_type=F32)


def call(kernel, outs, args, scratch=(), smem=0, far=None, far_outs=(), last=False):
    far = far or {}
    args = [
        x if i < smem
        else pltpu.with_memory_space_constraint(x, FAR if far.get(i, False) else pltpu.VMEM)
        for i, x in enumerate(args)
    ]
    shapes = []
    for i, out in enumerate(outs):
        make = jax.ShapeDtypeStruct if last or i in far_outs else pltpu.VMEM
        shapes.append(make(out, BF16) if isinstance(out, tuple) else out)
    return pl.pallas_call(
        kernel,
        out_shape=shapes,
        in_specs=[
            SMEM if i < smem else HBM if far.get(i, False) else VMEM for i in range(len(args))
        ],
        out_specs=[HBM if i in far_outs else VMEM for i in range(len(outs))],
        scratch_shapes=list(scratch),
    )(*args)


def combine_kernel(nbr_far, ham_far, out, nbr, ham, sems):
    fetches = [
        pltpu.make_async_copy(nbr_far, nbr, sems.at[0]),
        pltpu.make_async_copy(ham_far, ham, sems.at[1]),
    ]
    for fetch in fetches:
        fetch.start()
    for fetch in fetches:
        fetch.wait()
    blocks, slots = ham.shape[0], ham.shape[1]
    width = ham.shape[3]
    for r in range(blocks):
        layer = FACE + r // FACE * FACE
        for k, position in enumerate((r, layer, layer + 1, r + 2 * FACE)):
            total = jnp.zeros(ham.shape[2:], F32)
            for j in range(slots):
                keep = (nbr[r, j] == position).astype(F32)
                total = total + keep * ham[r, j].astype(F32)
            total = total.astype(BF16)
            for copy in range(out.shape[0]):
                out[copy, r, :, k * width : (k + 1) * width] = total


def product(ham, r, ext):
    tile = ham.shape[3] // 4
    layer = FACE + r // FACE * FACE
    rhs = jnp.concatenate(
        [
            ext[r * tile : (r + 1) * tile],
            ext[layer * tile : (layer + FACE) * tile],
            ext[(r + 2 * FACE) * tile : (r + 2 * FACE + 1) * tile],
        ],
        axis=0,
    )
    return dot(ham[:, r].reshape(tile, 4 * tile), rhs)


def fill(core, ext, vec, from_far, from_near):
    edge, rows = from_far.shape[0], vec.shape[0]
    c = core[0]
    ext[edge : edge + rows] = vec[...]
    ext[pl.ds(pl.multiple_of(c * (edge + rows), edge), edge)] = from_far[...]
    ext[pl.ds(pl.multiple_of((1 - c) * (edge + rows), edge), edge)] = from_near[...]


def step_kernel(prior, core, ham, vec, from_far, from_near, *rest):
    before = rest[0] if prior else None
    out, far, near, ext, *copying = rest[1:] if prior else rest
    if copying:
        out, copies, far, near, ext, sems = rest[1:]
    edge, rows = far.shape[0], vec.shape[0]
    tile = edge // FACE
    fill(core, ext, vec, from_far, from_near)
    for r in range(rows // tile):
        here = slice(r * tile, (r + 1) * tile)
        value = product(ham, r, ext)
        if prior:
            value = 2.0 * value - before[here].astype(F32)
        out[here] = value.astype(BF16)
    sends = []
    if copying:
        for i in range(copies.shape[0]):
            sends.append(pltpu.make_async_copy(out, copies.at[i], sems.at[i]))
    for send in sends:
        send.start()
    c = core[0]
    far[...] = out[pl.ds(pl.multiple_of(c * (rows - edge), edge), edge)]
    near[...] = out[pl.ds(pl.multiple_of((1 - c) * (rows - edge), edge), edge)]
    for send in sends:
        send.wait()


def inner_kernel(ham, vec, out, ext):
    rows = vec.shape[0]
    edge = (ext.shape[0] - rows) // 2
    tile = edge // FACE
    ext[edge : edge + rows] = vec[...]
    for i in range(out.shape[0] // tile):
        out[i * tile : (i + 1) * tile] = product(ham, FACE + i, ext).astype(BF16)


def outer_kernel(core, ham, vec, from_far, from_near, out, ext):
    edge, rows = from_far.shape[0], vec.shape[0]
    tile = edge // FACE
    fill(core, ext, vec, from_far, from_near)
    for i, r in enumerate((*range(FACE), *range(rows // tile - FACE, rows // tile))):
        out[i * tile : (i + 1) * tile] = product(ham, r, ext).astype(BF16)


def fetch_kernel(far, out, sem):
    fetch = pltpu.make_async_copy(far, out, sem.at[0])
    fetch.start()
    fetch.wait()


def gram_kernel(third, inner, outer, inner2, outer2, out):
    share, width = out.shape[1], third.shape[2]
    per = width // share
    edge = outer.shape[0] // 2
    own = jnp.concatenate([outer[:edge], inner[...], outer[edge:]], axis=0)
    other = jnp.concatenate([outer2[:edge], inner2[...], outer2[edge:]], axis=0)
    right = jnp.concatenate([own, other], axis=1)
    for y in range(third.shape[0]):
        block = dot(third[y], right, ((0,), (0,))).astype(BF16)
        for i in range(per):
            out[y * per + i] = block[i * share : (i + 1) * share]


def sum_kernel(scale, parts, out):
    total = parts[0].astype(F32)
    for i in range(1, parts.shape[0]):
        total = total + parts[i].astype(F32)
    if scale is not None:
        total = total * scale
    total = total.astype(BF16)
    for copy in range(out.shape[0]):
        out[copy] = total


def mixed_kernel(third, gram, inner, outer, out):
    strips, height, width = out.shape[0], out.shape[1], third.shape[2]
    count = third.shape[0]
    edge = outer.shape[0] // (2 * height)
    weights = gram[...].reshape(count * width, gram.shape[2])
    for s in range(strips):
        here = slice(s * height, (s + 1) * height)
        left = jnp.concatenate([third[y, here] for y in range(count)], axis=1)
        value = dot(left, weights)
        if s < edge:
            applied = outer[here]
        elif s < strips - edge:
            applied = inner[(s - edge) * height : (s - edge + 1) * height]
        else:
            at = (s - strips + 2 * edge) * height
            applied = outer[at : at + height]
        out[s, :, :width] = (applied.astype(F32) - value[:, :width]).astype(BF16)
        out[s, :, width:] = (-value[:, width:]).astype(BF16)


def final_kernel(parts, out):
    width = parts.shape[2] // 2
    for b in range(parts.shape[0]):
        value = parts[b, :, :width].astype(F32) + parts[b ^ 1, :, width:].astype(F32)
        out[:, b * width : (b + 1) * width] = value.astype(BF16)


def gather(copies, axes):
    return lax.all_to_all(copies, axes, 0, 0, tiled=True)


def swap(far, near):
    count = lax.axis_size(SLAB)
    pairs = [(s, (s + 1) % count if s % 2 else (s - 1) % count) for s in range(count)]
    from_far = lax.ppermute(far, SLAB, pairs)
    return from_far, lax.ppermute(near, "core", PAIR)


def filtered(hamiltonian, neighbors, orbitals):
    blocks, _, strip, tile = hamiltonian.shape
    rows, width = orbitals.shape
    edge = FACE * tile
    ny, nband, near, far = (lax.axis_size(a) for a in ("y", BAND, NEAR, FURTHER))
    core = lax.axis_index("core")
    scalar = core.astype(jnp.int32).reshape(1)

    (shares,) = call(
        combine_kernel,
        [(nband, blocks, strip, 4 * tile)],
        (neighbors, hamiltonian),
        (
            pltpu.SMEM(neighbors.shape, neighbors.dtype),
            pltpu.VMEM(hamiltonian.shape, BF16),
            pltpu.SemaphoreType.DMA((2,)),
        ),
        far={0: True, 1: True},
    )
    tiles = gather(shares, BAND)
    received = swap(
        lax.dynamic_slice_in_dim(orbitals, core * (rows - edge), edge, 0),
        lax.dynamic_slice_in_dim(orbitals, (1 - core) * (rows - edge), edge, 0),
    )

    ext = pltpu.VMEM((rows + 2 * edge, width), BF16)
    whole, face, part = (rows, width), (edge, width), (rows - 2 * edge, width)

    def step(vec, received, before=()):
        return call(
            functools.partial(step_kernel, bool(before)),
            [whole, face, face],
            (scalar, tiles, vec, *received, *before),
            (ext,),
            smem=1,
        )

    first, *faces = step(orbitals, received)
    second, *faces = step(first, swap(*faces), (orbitals,))
    third, copies, *faces = call(
        functools.partial(step_kernel, True),
        [whole, (ny, rows, width), face, face],
        (scalar, tiles, second, *swap(*faces), first),
        (ext, pltpu.SemaphoreType.DMA((ny,))),
        smem=1,
        far_outs=(1,),
    )
    received = swap(*faces)
    third_far = gather(copies, "y")
    (inner,) = call(inner_kernel, [part], (tiles, third), (ext,))
    inner2 = lax.ppermute(inner, "xl", PAIR)
    (outer,) = call(outer_kernel, [(2 * edge, width)], (scalar, tiles, third, *received), (ext,), smem=1)
    outer2 = lax.ppermute(outer, "xl", PAIR)
    (third_all,) = call(
        fetch_kernel,
        [(ny, rows, width)],
        (third_far,),
        (pltpu.SemaphoreType.DMA((1,)),),
        far={0: True},
    )

    rows_all = rows * lax.axis_size(SLAB)
    scale = 1.0 / math.sqrt(float(rows_all) * float(width * nband))
    columns = 2 * width
    share = ny * width // near
    (partial_gram,) = call(
        gram_kernel, [(near, share, columns)], (third_all, inner, outer, inner2, outer2)
    )
    (summed,) = call(
        functools.partial(sum_kernel, None), [(far, share, columns)], (gather(partial_gram, NEAR),)
    )
    (scaled,) = call(
        functools.partial(sum_kernel, scale), [(near, share, columns)], (gather(summed, FURTHER),)
    )
    gram = gather(scaled, NEAR)
    (partial_out,) = call(
        mixed_kernel,
        [(nband, rows // nband, columns)],
        (third_all, gram, inner, outer),
    )
    (out,) = call(
        final_kernel, [(rows // nband, nband * width)], (gather(partial_out, BAND),), last=True
    )
    return out


def solution(mesh):
    slabs = mesh.shape["slab"]
    fine = Mesh(
        np.asarray(mesh.devices).reshape(slabs // 16, 4, 2, 2, mesh.shape["band"] // 2, 2),
        SLAB + BAND,
    )
    in_specs = (P(SLAB, None, BAND, None), P(SLAB, None), P(SLAB, BAND))
    out_specs = P(SLAB + BAND, None)
    return jax.shard_map(filtered, mesh=fine, in_specs=in_specs, out_specs=out_specs, check_vma=False)
```

```python
import functools
import math

import jax
import jax.numpy as jnp
import numpy as np
from jax import lax
from jax.experimental import pallas as pl
from jax.experimental.pallas import tpu as pltpu
from jax.sharding import Mesh
from jax.sharding import PartitionSpec as P

SLAB = ("z2", "z1", "xh", "core")
BAND = ("y", "xl")
NEAR = ("z1", "xh", "core")
PAIR = [(0, 1), (1, 0)]
FACE = 2
F32 = jnp.float32
BF16 = jnp.bfloat16

VMEM = pl.BlockSpec(memory_space=pltpu.VMEM)
SMEM = pl.BlockSpec(memory_space=pltpu.SMEM)
FAR = pltpu.MemorySpace.HBM
HBM = pl.BlockSpec(memory_space=FAR)


def dot(a, b, dims=((1,), (0,))):
    return lax.dot_general(a, b, (dims, ((), ())), preferred_element_type=F32)


def call(kernel, outs, args, scratch=(), smem=0, far=None, far_outs=(), last=False):
    far = far or {}
    args = [
        x if i < smem
        else pltpu.with_memory_space_constraint(x, FAR if far.get(i, False) else pltpu.VMEM)
        for i, x in enumerate(args)
    ]
    shapes = []
    for i, out in enumerate(outs):
        make = jax.ShapeDtypeStruct if last or i in far_outs else pltpu.VMEM
        shapes.append(make(out, BF16) if isinstance(out, tuple) else out)
    return pl.pallas_call(
        kernel,
        out_shape=shapes,
        in_specs=[
            SMEM if i < smem else HBM if far.get(i, False) else VMEM for i in range(len(args))
        ],
        out_specs=[HBM if i in far_outs else VMEM for i in range(len(outs))],
        scratch_shapes=list(scratch),
    )(*args)


def combine_kernel(nbr_far, ham_far, out, nbr, ham, sems):
    fetches = [
        pltpu.make_async_copy(nbr_far, nbr, sems.at[0]),
        pltpu.make_async_copy(ham_far, ham, sems.at[1]),
    ]
    for fetch in fetches:
        fetch.start()
    for fetch in fetches:
        fetch.wait()
    blocks, slots = ham.shape[0], ham.shape[1]
    width = ham.shape[3]
    for r in range(blocks):
        layer = FACE + r // FACE * FACE
        for k, position in enumerate((r, layer, layer + 1, r + 2 * FACE)):
            total = jnp.zeros(ham.shape[2:], F32)
            for j in range(slots):
                keep = (nbr[r, j] == position).astype(F32)
                total = total + keep * ham[r, j].astype(F32)
            total = total.astype(BF16)
            for copy in range(out.shape[0]):
                out[copy, r, :, k * width : (k + 1) * width] = total


def product(ham, r, ext):
    tile = ham.shape[3] // 4
    layer = FACE + r // FACE * FACE
    rhs = jnp.concatenate(
        [
            ext[r * tile : (r + 1) * tile],
            ext[layer * tile : (layer + FACE) * tile],
            ext[(r + 2 * FACE) * tile : (r + 2 * FACE + 1) * tile],
        ],
        axis=0,
    )
    return dot(ham[:, r].reshape(tile, 4 * tile), rhs)


def fill(ext, inner, outer):
    edge, rows = outer.shape[0] // 2, inner.shape[0]
    ext[edge : 2 * edge] = outer[:edge]
    ext[2 * edge : 2 * edge + rows] = inner[...]
    ext[2 * edge + rows : 3 * edge + rows] = outer[edge:]


def inner_kernel(prior, ham, inner, outer, *rest):
    out, ext = rest[-2:]
    tile = ham.shape[3] // 4
    fill(ext, inner, outer)
    for i in range(out.shape[0] // tile):
        here = slice(i * tile, (i + 1) * tile)
        value = product(ham, FACE + i, ext)
        if prior:
            value = 2.0 * value - rest[0][here].astype(F32)
        out[here] = value.astype(BF16)


def outer_kernel(prior, copying, core, ham, inner, outer, from_far, from_near, *rest):
    rest = list(rest)
    before = rest.pop(0) if prior else None
    done = rest.pop(0) if copying else None
    out = rest.pop(0)
    copies = rest.pop(0) if copying else None
    ext = rest[-2] if copying else rest[-1]
    sems = rest[-1]
    edge, rows = from_far.shape[0], inner.shape[0]
    tile = edge // FACE
    sends = []

    def send(part, start, which):
        for i in range(copies.shape[0]):
            here = pl.ds(start, part.shape[0])
            sends.append(pltpu.make_async_copy(part, copies.at[i, here], sems.at[which, i]))
            sends[-1].start()

    if copying:
        send(done, 0, 0)
    fill(ext, inner, outer)
    c = core[0]
    last = rows + 3 * edge
    ext[pl.ds(pl.multiple_of(c * last, edge), edge)] = from_far[...]
    ext[pl.ds(pl.multiple_of((1 - c) * last, edge), edge)] = from_near[...]
    blocks = (rows + 2 * edge) // tile
    for i, r in enumerate((*range(FACE), *range(blocks - FACE, blocks))):
        here = slice(i * tile, (i + 1) * tile)
        value = product(ham, r, ext)
        if prior:
            value = 2.0 * value - before[here].astype(F32)
        out[here] = value.astype(BF16)
    if copying:
        send(out, rows, 1)
    if len(rest) > 1:
        rest[0][...] = out[pl.ds(pl.multiple_of(c * edge, edge), edge)]
        rest[1][...] = out[pl.ds(pl.multiple_of((1 - c) * edge, edge), edge)]
    for copy in sends:
        copy.wait()


def fetch_kernel(far, out, sem):
    fetch = pltpu.make_async_copy(far, out, sem.at[0])
    fetch.start()
    fetch.wait()


def gram_kernel(third, inner, outer, inner2, outer2, out):
    share, width = out.shape[1], third.shape[2]
    per = width // share
    own = jnp.concatenate([inner[...], outer[...]], axis=0)
    other = jnp.concatenate([inner2[...], outer2[...]], axis=0)
    right = jnp.concatenate([own, other], axis=1)
    for y in range(third.shape[0]):
        block = dot(third[y], right, ((0,), (0,))).astype(BF16)
        for i in range(per):
            out[y * per + i] = block[i * share : (i + 1) * share]


def sum_kernel(scale, parts, out):
    total = parts[0].astype(F32)
    for i in range(1, parts.shape[0]):
        total = total + parts[i].astype(F32)
    if scale is not None:
        total = total * scale
    total = total.astype(BF16)
    for copy in range(out.shape[0]):
        out[copy] = total


def mixed_kernel(third, gram, inner, outer, out):
    strips, height, width = out.shape[0], out.shape[1], third.shape[2]
    count = third.shape[0]
    edge = outer.shape[0] // (2 * height)
    weights = gram[...].reshape(count * width, gram.shape[2])
    for s in range(strips):
        part, at = inner, (s - edge) * height
        if s < edge or s >= strips - edge:
            part, at = outer, (s if s < edge else s - strips + 2 * edge) * height
        here = slice(at, at + height)
        start = at + (0 if part is inner else inner.shape[0])
        left = jnp.concatenate(
            [third[y, start : start + height] for y in range(count)], axis=1
        )
        value = dot(left, weights)
        applied = part[here]
        out[s, :, :width] = (applied.astype(F32) - value[:, :width]).astype(BF16)
        out[s, :, width:] = (-value[:, width:]).astype(BF16)


def final_kernel(parts, out):
    width = parts.shape[2] // 2
    for b in range(parts.shape[0]):
        value = parts[b, :, :width].astype(F32) + parts[b ^ 1, :, width:].astype(F32)
        out[:, b * width : (b + 1) * width] = value.astype(BF16)


def gather(copies, axes):
    return lax.all_to_all(copies, axes, 0, 0, tiled=True)


def swap(far, near):
    count = lax.axis_size(SLAB)
    pairs = [(s, (s + 1) % count if s % 2 else (s - 1) % count) for s in range(count)]
    from_far = lax.ppermute(far, SLAB, pairs)
    return from_far, lax.ppermute(near, "core", PAIR)


def filtered(hamiltonian, neighbors, orbitals):
    blocks, _, strip, tile = hamiltonian.shape
    rows, width = orbitals.shape
    edge = FACE * tile
    ny, nband, near, far = (lax.axis_size(a) for a in ("y", BAND, NEAR, "z2"))
    core = lax.axis_index("core")
    scalar = core.astype(jnp.int32).reshape(1)

    (shares,) = call(
        combine_kernel,
        [(nband, blocks, strip, 4 * tile)],
        (neighbors, hamiltonian),
        (
            pltpu.SMEM(neighbors.shape, neighbors.dtype),
            pltpu.VMEM(hamiltonian.shape, BF16),
            pltpu.SemaphoreType.DMA((2,)),
        ),
        far={0: True, 1: True},
    )
    tiles = gather(shares, BAND)
    received = swap(
        lax.dynamic_slice_in_dim(orbitals, core * (rows - edge), edge, 0),
        lax.dynamic_slice_in_dim(orbitals, (1 - core) * (rows - edge), edge, 0),
    )

    ext = pltpu.VMEM((rows + 2 * edge, width), BF16)
    face, inside, outside = (edge, width), (rows - 2 * edge, width), (2 * edge, width)

    def step_inner(vec, before=()):
        kernel = functools.partial(inner_kernel, bool(before))
        return call(kernel, [inside], (tiles, *vec, *before), (ext,))[0]

    def step_outer(vec, received, before=(), done=(), faces=True):
        outs = [outside] + ([(ny, rows, width)] if done else []) + ([face, face] if faces else [])
        return call(
            functools.partial(outer_kernel, bool(before), bool(done)),
            outs,
            (scalar, tiles, *vec, *received, *before, *done),
            (ext, pltpu.SemaphoreType.DMA((2, ny))) if done else (ext,),
            smem=1,
            far_outs=(1,) if done else (),
        )

    start = (
        orbitals[edge : rows - edge],
        jnp.concatenate([orbitals[:edge], orbitals[rows - edge :]], axis=0),
    )
    first_outer, *faces = step_outer(start, received)
    received = swap(*faces)
    first = (step_inner(start), first_outer)
    second_inner = step_inner(first, start[:1])
    second_outer, *faces = step_outer(first, received, start[1:])
    received = swap(*faces)
    second = (second_inner, second_outer)
    third_inner = step_inner(second, first[:1])
    third_outer, copies, *faces = step_outer(second, received, first[1:], (third_inner,))
    received = swap(*faces)
    third = (third_inner, third_outer)
    third_far = gather(copies, "y")
    inner = step_inner(third)
    inner2 = lax.ppermute(inner, "xl", PAIR)
    (outer,) = step_outer(third, received, faces=False)
    outer2 = lax.ppermute(outer, "xl", PAIR)
    (third_all,) = call(
        fetch_kernel,
        [(ny, rows, width)],
        (third_far,),
        (pltpu.SemaphoreType.DMA((1,)),),
        far={0: True},
    )

    rows_all = rows * lax.axis_size(SLAB)
    scale = 1.0 / math.sqrt(float(rows_all) * float(width * nband))
    columns = 2 * width
    share = ny * width // near
    (partial_gram,) = call(
        gram_kernel, [(near, share, columns)], (third_all, inner, outer, inner2, outer2)
    )
    (summed,) = call(
        functools.partial(sum_kernel, None), [(far, share, columns)], (gather(partial_gram, NEAR),)
    )
    (scaled,) = call(
        functools.partial(sum_kernel, scale), [(near, share, columns)], (gather(summed, "z2"),)
    )
    gram = gather(scaled, NEAR)
    (partial_out,) = call(
        mixed_kernel,
        [(nband, rows // nband, columns)],
        (third_all, gram, inner, outer),
    )
    (out,) = call(
        final_kernel, [(rows // nband, nband * width)], (gather(partial_out, BAND),), last=True
    )
    return out


def solution(mesh):
    slabs = mesh.shape["slab"]
    fine = Mesh(
        np.asarray(mesh.devices).reshape(slabs // 16, 4, 2, 2, mesh.shape["band"] // 2, 2),
        SLAB + BAND,
    )
    in_specs = (P(SLAB, None, BAND, None), P(SLAB, None), P(SLAB, BAND))
    out_specs = P(SLAB + BAND, None)
    return jax.shard_map(filtered, mesh=fine, in_specs=in_specs, out_specs=out_specs, check_vma=False)
```
